32 devices in a mesh: row: 4 (over y, x), col: 8 (over z, core).
Axes of the slice: x: 2, y: 2, z: 4, core: 2. Of those that a mesh axis runs over, the one named last changes fastest.
Arguments:
- vectors: float32 [4608, 4096], P('row', 'col'), may hold values from -6 to 6
- reflectors: float32 [256, 2304], P('col', 'row'), may hold values from -0.75 to 0.75
Outputs:
- result: float32 [4608, 4096], P('row', 'col')
The draws below stay inside these ranges and needn't reach their ends.
All inputs are finite; a program needn't handle non-finite values.
Results may differ from the reference program's by a relative error of at most 0.00019.
Values sent between devices are 32-bit elements; how exact they have to be, the bound alone decides.
A program may use at most 64 MiB of HBM per device.

```python
import jax
import jax.numpy as jnp
from jax import lax

BAND = 64
GROUPS = 4
ROWS = 4608
COLS = 4096
REFLS = 256


def levels(own_key, extent, shards, smallest, high):
    level, own = 1.0, jax.random.fold_in(own_key, 6)
    for axis_at, parts in shards:
        heights = jnp.exp(jax.random.uniform(jax.random.fold_in(own, axis_at), (parts,), jnp.float32, smallest / len(shards), high / len(shards)))
        level = level * jnp.repeat(heights, extent[axis_at] // parts).reshape([-1 if axis == axis_at else 1 for axis in range(len(extent))])
    return level


def gaussian(own_key, shape, width, reach, shards=(), kind=jnp.bfloat16):
    array = width * jax.random.normal(own_key, shape, jnp.float32)
    if shards:
        array = array * levels(own_key, shape, shards, -0.22, 0.18)
    return jnp.clip(array, -reach, reach).astype(kind)


def setup_inputs(seed: int = 0) -> dict:
    key_of = jax.random.split(jax.random.key(seed), 3)
    vectors = gaussian(key_of[0], (ROWS, COLS), 1.0, 6.0, ((0, 4), (1, 8)), jnp.float32)
    reflectors = gaussian(key_of[1], (REFLS, ROWS // 2), BAND ** -0.5, 0.75, ((0, 8), (1, 4)), jnp.float32)
    return dict(vectors=vectors, reflectors=reflectors)


def upper_inverse(upper):
    diag_part = jnp.diagonal(upper, axis1=1, axis2=2)
    identity = jnp.eye(BAND, dtype=jnp.float32)
    nilpotent = upper / diag_part[:, :, None] - identity
    power = nilpotent
    inverse = identity - nilpotent
    for level in range(5):
        power = jnp.einsum("wab,wbc->wac", power, power, precision=lax.Precision.HIGHEST)
        inverse = jnp.einsum("wab,wbc->wac", inverse, identity + power, precision=lax.Precision.HIGHEST)
    return inverse / diag_part[:, None, :]


def reflector_blocks(compact):
    windows = compact.shape[0]
    column = lax.broadcasted_iota(jnp.int32, compact.shape, 2)
    filled = jnp.where(column == 0, jnp.float32(1.0), compact)
    padded = jnp.pad(filled, ((0, 0), (0, 0), (0, BAND + 1)))
    skewed = padded.reshape(windows, BAND * (2 * BAND + 1))[:, :2 * BAND * BAND].reshape(windows, BAND, 2 * BAND)
    gram_matrix = jnp.einsum("wji,wli->wjl", skewed, skewed, precision=lax.Precision.HIGHEST)
    upper_inv = jnp.triu(gram_matrix, 1) + 0.5 * gram_matrix * jnp.eye(BAND, dtype=jnp.float32)
    return skewed, upper_inverse(upper_inv)


def reflect_windows(blocks, skewed, inverse, weight):
    inner_prod = jnp.einsum("wji,wic->wjc", skewed, blocks, precision=lax.Precision.HIGHEST)
    solved = jnp.einsum("wjl,wlc->wjc", inverse, inner_prod, precision=lax.Precision.HIGHEST)
    change = jnp.einsum("wji,wjc->wic", skewed, solved, precision=lax.Precision.HIGHEST)
    return blocks - weight[:, None, None] * change


def reference(vectors, reflectors):
    all_rows = vectors.shape[0]
    result = vectors
    for group_index in range(GROUPS):
        offset = BAND * (group_index % 2)
        windows = (all_rows - offset) // (2 * BAND)
        compact = reflectors[group_index * BAND:(group_index + 1) * BAND, :windows * BAND]
        compact = compact.reshape(BAND, windows, BAND).transpose(1, 0, 2)
        skewed, inverse = reflector_blocks(compact)
        blocks = result[offset:offset + windows * 2 * BAND].reshape(windows, 2 * BAND, -1)
        blocks = reflect_windows(blocks, skewed, inverse, jnp.ones((windows,), jnp.float32))
        result = jnp.concatenate([result[:offset], blocks.reshape(windows * 2 * BAND, -1), result[offset + windows * 2 * BAND:]], 0)
    return result
```

```python
import functools

import jax
import jax.numpy as jnp
from jax import lax
from jax.experimental import pallas as pl
from jax.experimental.pallas import tpu as pltpu
from jax.sharding import PartitionSpec as P

BAND = 64
GROUPS = 4
WIN = 2 * BAND
HALO = GROUPS * BAND
SIDE = GROUPS // 2


def group_range(group, own):
    return group // 2, own + GROUPS - group


def split(x):
    high = x.astype(jnp.bfloat16)
    low = (x - high.astype(jnp.float32)).astype(jnp.bfloat16)
    return high, low


def dot(a, b, dims=(1, 0)):
    return lax.dot_general(
        a, b, (((dims[0],), (dims[1],)), ((), ())), preferred_element_type=jnp.float32
    )


def product(a, b):
    ah, al = split(a)
    bh, bl = split(b)
    return dot(jnp.concatenate([ah, al], 1), jnp.concatenate([bh, bh], 0)) + dot(ah, bl)


def prep_kernel(own, all_windows, refl_ref, q_ref):
    group = pl.program_id(0)
    first = lax.axis_index("row") * own - SIDE
    size = WIN
    held = own + 2 * SIDE
    pairs = (held + 1) // 2
    row = lax.broadcasted_iota(jnp.int32, (size, size), 0)
    lane = lax.broadcasted_iota(jnp.int32, (size, size), 1)
    eye = row == lane
    identity = eye.astype(jnp.float32)
    upper = (row // BAND == lane // BAND) & (row < lane)
    inside = (row // BAND) == (lane // BAND)
    lead = inside & (lane % BAND == 0)

    skews, nils, invs, scaled = [], [], [], []
    for pair in range(pairs):
        if (pair + 1) * size <= held * BAND:
            slab = refl_ref[:, pair * size : (pair + 1) * size]
        else:
            part = refl_ref[:, pair * size : pair * size + BAND]
            slab = jnp.concatenate([part, jnp.zeros_like(part)], 1)
        both = jnp.concatenate([slab, slab], 0)
        both = jnp.where(lead, 1.0, jnp.where(inside, both, 0.0))
        skews.append(pltpu.roll(both, 0, 1, stride=1, stride_axis=0))
    for pair in range(pairs):
        high, low = split(skews[pair])
        gram = dot(
            jnp.concatenate([high, low], 1), jnp.concatenate([high, high], 1), (1, 1)
        ) + dot(high, low, (1, 1))
        diag = 0.5 * jnp.sum(jnp.where(eye, gram, 0.0), axis=1, keepdims=True)
        scale = 1.0 / diag
        nils.append(jnp.where(upper, gram * scale, 0.0))
        scaled.append(skews[pair] * scale)
    block = BAND // 4
    near = row // block == lane // block
    powers = [jnp.where(near, n, 0.0) for n in nils]
    invs = [identity - p for p in powers]
    powers = [product(p, p) for p in powers]
    for level in range(2):
        stacked = [product(jnp.concatenate([i, p], 0), p) for i, p in zip(invs, powers)]
        invs = [i + s[:size] for i, s in zip(invs, stacked)]
        powers = [s[size:] for s in stacked]
    invs = [i + product(i, p) for i, p in zip(invs, powers)]
    for _ in range(2):
        wide = row // (2 * block) == lane // (2 * block)
        far = wide & (row // block != lane // block)
        cross = [product(jnp.where(far, n, 0.0), i) for n, i in zip(nils, invs)]
        invs = [i - product(i, c) for i, c in zip(invs, cross)]
        block *= 2
    solved = [product(i, s) for i, s in zip(invs, scaled)]
    usable = all_windows - group % 2
    for pair in range(pairs):
        sh, sl = split(skews[pair])
        th, tl = split(solved[pair])
        for half in range(2):
            k = 2 * pair + half
            if k >= held:
                continue
            at = slice(half * BAND, (half + 1) * BAND)
            left = jnp.concatenate([sh[at], sl[at], sh[at]], 0)
            right = jnp.concatenate([th[at], th[at], tl[at]], 0)
            change = dot(left, right, (0, 0))
            window = first + k
            weight = ((window >= 0) & (window < usable)).astype(jnp.float32)
            high, low = split(identity - weight * change)
            q_ref[0, k, :, :size] = high
            q_ref[0, k, :, size:] = low


def apply_kernel(own, q_ref, above_ref, x_ref, below_ref, out_ref, work_ref):
    rows = x_ref.shape[0]
    for group in range(GROUPS):
        start, count = group_range(group, own)
        for k in range(start, start + count):
            at = BAND * (group % 2) + WIN * k
            if group == 0:
                if at < HALO:
                    block = above_ref[at : at + WIN, :]
                elif at < HALO + rows:
                    block = x_ref[at - HALO : at - HALO + WIN, :]
                else:
                    block = below_ref[at - HALO - rows : at - HALO - rows + WIN, :]
            else:
                block = work_ref[at : at + WIN, :]
            xh, xl = split(block)
            q = q_ref[group, k]
            new = dot(q, jnp.concatenate([xh, xh], 0)) + dot(q[:, :WIN], xl)
            if group < GROUPS - 1:
                work_ref[at : at + WIN, :] = new
            else:
                low, high = max(at, HALO), min(at + WIN, HALO + rows)
                out_ref[low - HALO : high - HALO, :] = new[low - at : high - at, :]


def shards(vectors, reflectors):
    rows, columns = vectors.shape
    own = rows // WIN
    count = lax.axis_size("row")
    forward = [(i, i + 1) for i in range(count - 1)]
    backward = [(i + 1, i) for i in range(count - 1)]
    width = SIDE * BAND
    before = lax.ppermute(reflectors[:, reflectors.shape[1] - width :], "row", forward)
    after = lax.ppermute(reflectors[:, :width], "row", backward)
    above = lax.ppermute(vectors[rows - HALO :], "row", forward)
    below = lax.ppermute(vectors[:HALO], "row", backward)
    stored = jnp.concatenate([before, reflectors, after], 1)
    everything = lax.all_gather(stored, "col", axis=0, tiled=True)

    held = own + 2 * SIDE
    q = pl.pallas_call(
        functools.partial(prep_kernel, own, own * count),
        grid=(GROUPS,),
        in_specs=[pl.BlockSpec((BAND, held * BAND), lambda g: (g, 0))],
        out_specs=pl.BlockSpec((1, held, WIN, 2 * WIN), lambda g: (g, 0, 0, 0)),
        out_shape=jax.ShapeDtypeStruct((GROUPS, held, WIN, 2 * WIN), jnp.bfloat16),
        cost_estimate=pl.CostEstimate(
            flops=GROUPS * held * 60 * WIN**3, bytes_accessed=2**22, transcendentals=0
        ),
        name="prep",
    )(everything)
    tile = min(columns, 256)
    return pl.pallas_call(
        functools.partial(apply_kernel, own),
        grid=(columns // tile,),
        in_specs=[
            pl.BlockSpec(q.shape, lambda c: (0, 0, 0, 0)),
            pl.BlockSpec((HALO, tile), lambda c: (0, c)),
            pl.BlockSpec((rows, tile), lambda c: (0, c)),
            pl.BlockSpec((HALO, tile), lambda c: (0, c)),
        ],
        out_specs=pl.BlockSpec((rows, tile), lambda c: (0, c)),
        out_shape=jax.ShapeDtypeStruct(vectors.shape, vectors.dtype),
        scratch_shapes=[pltpu.VMEM((rows + 2 * HALO, tile), jnp.float32)],
        name="apply",
    )(q, above, vectors, below)


def solution(mesh):
    placed = (P("row", "col"), P("col", "row"))
    return jax.shard_map(
        shards, mesh=mesh, in_specs=placed, out_specs=P("row", "col"), check_vma=False
    )
```

```python
import functools

import jax
import jax.numpy as jnp
from jax import lax
from jax.experimental import pallas as pl
from jax.experimental.pallas import tpu as pltpu
from jax.sharding import PartitionSpec as P

BAND = 64
GROUPS = 4
WIN = 2 * BAND
HALO = GROUPS * BAND
SIDE = GROUPS // 2


def group_range(group, own):
    return group // 2, own + GROUPS - group


def split(x):
    high = x.astype(jnp.bfloat16)
    low = (x - high.astype(jnp.float32)).astype(jnp.bfloat16)
    return high, low


def dot(a, b, dims=(1, 0)):
    return lax.dot_general(
        a, b, (((dims[0],), (dims[1],)), ((), ())), preferred_element_type=jnp.float32
    )


def product(a, b):
    ah, al = split(a)
    bh, bl = split(b)
    return dot(jnp.concatenate([ah, al], 1), jnp.concatenate([bh, bh], 0)) + dot(ah, bl)


def build_group(own, all_windows, group, refl, q_ref):
    first = lax.axis_index("row") * own - SIDE
    size = WIN
    held = own + 2 * SIDE
    pairs = (held + 1) // 2
    row = lax.broadcasted_iota(jnp.int32, (size, size), 0)
    lane = lax.broadcasted_iota(jnp.int32, (size, size), 1)
    eye = row == lane
    identity = eye.astype(jnp.float32)
    upper = (row // BAND == lane // BAND) & (row < lane)
    inside = (row // BAND) == (lane // BAND)
    lead = inside & (lane % BAND == 0)

    skews, nils, invs, scaled = [], [], [], []
    for pair in range(pairs):
        if (pair + 1) * size <= held * BAND:
            slab = refl[:, pair * size : (pair + 1) * size]
        else:
            part = refl[:, pair * size : pair * size + BAND]
            slab = jnp.concatenate([part, jnp.zeros_like(part)], 1)
        both = jnp.concatenate([slab, slab], 0)
        both = jnp.where(lead, 1.0, jnp.where(inside, both, 0.0))
        skews.append(pltpu.roll(both, 0, 1, stride=1, stride_axis=0))
    for pair in range(pairs):
        high, low = split(skews[pair])
        gram = dot(
            jnp.concatenate([high, low], 1), jnp.concatenate([high, high], 1), (1, 1)
        ) + dot(high, low, (1, 1))
        diag = 0.5 * jnp.sum(jnp.where(eye, gram, 0.0), axis=1, keepdims=True)
        scale = 1.0 / diag
        nils.append(jnp.where(upper, gram * scale, 0.0))
        scaled.append(skews[pair] * scale)
    block = BAND // 4
    near = row // block == lane // block
    powers = [jnp.where(near, n, 0.0) for n in nils]
    invs = [identity - p for p in powers]
    powers = [product(p, p) for p in powers]
    for level in range(2):
        stacked = [product(jnp.concatenate([i, p], 0), p) for i, p in zip(invs, powers)]
        invs = [i + s[:size] for i, s in zip(invs, stacked)]
        powers = [s[size:] for s in stacked]
    invs = [i + product(i, p) for i, p in zip(invs, powers)]
    for _ in range(2):
        wide = row // (2 * block) == lane // (2 * block)
        far = wide & (row // block != lane // block)
        cross = [product(jnp.where(far, n, 0.0), i) for n, i in zip(nils, invs)]
        invs = [i - product(i, c) for i, c in zip(invs, cross)]
        block *= 2
    solved = [product(i, s) for i, s in zip(invs, scaled)]
    usable = all_windows - group % 2
    for pair in range(pairs):
        sh, sl = split(skews[pair])
        th, tl = split(solved[pair])
        for half in range(2):
            k = 2 * pair + half
            if k >= held:
                continue
            at = slice(half * BAND, (half + 1) * BAND)
            left = jnp.concatenate([sh[at], sl[at], sh[at]], 0)
            right = jnp.concatenate([th[at], th[at], tl[at]], 0)
            change = dot(left, right, (0, 0))
            window = first + k
            weight = ((window >= 0) & (window < usable)).astype(jnp.float32)
            high, low = split(identity - weight * change)
            q_ref[group, k, :, :size] = high
            q_ref[group, k, :, size:] = low


def mixed(a, b, count):
    total, bit = 0, 1
    while bit < count:
        total = total + ((a // bit + b // bit) % 2) * bit
        bit *= 2
    return total


def gather_kernel(
    own, rows_axis, cols_axis, refl_ref, head_ref, tail_ref, x_ref,
    q_ref, above_ref, below_ref,
    main, left, right, near_send, near_recv, line_send, line_recv, pair_send, pair_recv, own_sem,
):
    row, me = lax.axis_index("row"), lax.axis_index("col")
    chips = cols_axis // 2
    chip, core = me // 2, me % 2
    up, down = (row + rows_axis - 1) % rows_axis, (row + 1) % rows_axis
    other = chip * 2 + 1 - core
    rows = x_ref.shape[0]
    mesh_ids = pl.DeviceIdType.MESH

    barrier = pltpu.get_barrier_semaphore()
    partners = [(row, mixed(chip, i, chips) * 2 + core) for i in range(1, chips)]
    partners += [(row, other), (up, me), (down, me)]
    for partner in partners:
        pl.semaphore_signal(barrier, inc=1, device_id=partner, device_id_type=mesh_ids)
    pl.semaphore_wait(barrier, len(partners))

    def remote(source, target, send, recv, device):
        return pltpu.make_async_remote_copy(
            src_ref=source, dst_ref=target, send_sem=send, recv_sem=recv,
            device_id=device, device_id_type=mesh_ids,
        )

    slots = (main, left, right)
    pending = []

    def share(kind, source):
        pair = remote(source, slots[kind].at[me], pair_send.at[kind, chip], pair_recv.at[kind, chip], (row, other))
        pair.start()
        pending.append(pair)
        for i in range(1, chips):
            there = mixed(chip, i, chips)
            line = remote(source, slots[kind].at[me], line_send.at[kind, there], line_recv.at[kind, chip], (row, there * 2 + core))
            line.start()
            pending.append(line)

    near = [
        remote(tail_ref, left.at[me], near_send.at[0], near_recv.at[0], (down, me)),
        remote(head_ref, right.at[me], near_send.at[1], near_recv.at[1], (up, me)),
    ]
    for copy in near:
        copy.start()
    local = pltpu.make_async_copy(refl_ref, main.at[me], own_sem)
    local.start()
    share(0, refl_ref)
    halos = [
        remote(x_ref.at[pl.ds(rows - HALO, HALO)], above_ref, near_send.at[2], near_recv.at[2], (down, me)),
        remote(x_ref.at[pl.ds(0, HALO)], below_ref, near_send.at[3], near_recv.at[3], (up, me)),
    ]
    for copy in halos:
        copy.start()
    for kind, copy in zip((1, 2), near):
        copy.wait_recv()
        share(kind, slots[kind].at[me])
    local.wait()

    def arrived(kind, there, mine, recv):
        slot = slots[kind].at[there * 2 + (core if mine else 1 - core)]
        remote(slot, slot, own_sem, recv.at[kind, there], (row, other)).wait_recv()

    share_group = cols_axis // GROUPS
    chip_group = share_group // 2
    mine = chip // chip_group

    def members(i):
        base = mixed(mine, i, GROUPS) * chip_group
        return [base + mixed(chip % chip_group, j, chip_group) for j in range(chip_group)]

    def forward(i):
        for j, there in enumerate(members(i)):
            if i == 0 and j == 0:
                continue
            for kind in range(3):
                arrived(kind, there, True, line_recv)
                slot = slots[kind].at[there * 2 + core]
                copy = remote(slot, slot, pair_send.at[kind, there], pair_recv.at[kind, there], (row, other))
                copy.start()
                pending.append(copy)

    def build(i):
        for there in members(i):
            for kind in range(3):
                arrived(kind, there, False, pair_recv)
        group = mixed(mine, i, GROUPS)
        parts = [slot[pl.ds(group * share_group, share_group)] for slot in (left, main, right)]
        refl = jnp.concatenate([p.reshape(BAND, p.shape[2]) for p in parts], 1)
        build_group(own, own * rows_axis, group, refl, q_ref)

    forward(0)
    build(0)
    forward(1)
    for i in range(1, GROUPS):
        if i + 1 < GROUPS:
            forward(i + 1)
        build(i)
    for copy in halos:
        copy.wait()
    for copy in near:
        copy.wait_send()
    for copy in pending:
        copy.wait_send()


def apply_kernel(own, q_ref, above_ref, x_ref, below_ref, out_ref, work_ref):
    rows = x_ref.shape[0]
    for group in range(GROUPS):
        start, count = group_range(group, own)
        for k in range(start, start + count):
            at = BAND * (group % 2) + WIN * k
            if group == 0:
                if at < HALO:
                    block = above_ref[at : at + WIN, :]
                elif at < HALO + rows:
                    block = x_ref[at - HALO : at - HALO + WIN, :]
                else:
                    block = below_ref[at - HALO - rows : at - HALO - rows + WIN, :]
            else:
                block = work_ref[at : at + WIN, :]
            xh, xl = split(block)
            q = q_ref[group, k]
            new = dot(q, jnp.concatenate([xh, xh], 0)) + dot(q[:, :WIN], xl)
            if group < GROUPS - 1:
                work_ref[at : at + WIN, :] = new
            else:
                low, high = max(at, HALO), min(at + WIN, HALO + rows)
                out_ref[low - HALO : high - HALO, :] = new[low - at : high - at, :]


def shards(vectors, reflectors):
    rows, columns = vectors.shape
    own = rows // WIN
    rows_axis, cols_axis = lax.axis_size("row"), lax.axis_size("col")
    width = SIDE * BAND
    slots, stored = reflectors.shape
    head, tail = reflectors[:, :width], reflectors[:, stored - width :]
    held = own + 2 * SIDE
    anywhere = pl.BlockSpec(memory_space=pl.ANY)
    halo = jax.ShapeDtypeStruct((HALO, columns), vectors.dtype)
    dma = pltpu.SemaphoreType.DMA
    q, above, below = pl.pallas_call(
        functools.partial(gather_kernel, own, rows_axis, cols_axis),
        in_specs=[anywhere] * 4,
        out_specs=[pl.BlockSpec(memory_space=pltpu.VMEM), anywhere, anywhere],
        out_shape=[jax.ShapeDtypeStruct((GROUPS, held, WIN, 2 * WIN), jnp.bfloat16), halo, halo],
        scratch_shapes=[
            pltpu.VMEM((cols_axis, slots, stored), jnp.float32),
            pltpu.VMEM((cols_axis, slots, width), jnp.float32),
            pltpu.VMEM((cols_axis, slots, width), jnp.float32),
            dma((4,)),
            dma((4,)),
            dma((3, cols_axis // 2)),
            dma((3, cols_axis // 2)),
            dma((3, cols_axis // 2)),
            dma((3, cols_axis // 2)),
            dma,
        ],
        compiler_params=pltpu.CompilerParams(collective_id=0, has_side_effects=True),
        name="gather",
    )(reflectors, head, tail, vectors)
    tile = min(columns, 256)
    return pl.pallas_call(
        functools.partial(apply_kernel, own),
        grid=(columns // tile,),
        in_specs=[
            pl.BlockSpec(q.shape, lambda c: (0, 0, 0, 0)),
            pl.BlockSpec((HALO, tile), lambda c: (0, c)),
            pl.BlockSpec((rows, tile), lambda c: (0, c)),
            pl.BlockSpec((HALO, tile), lambda c: (0, c)),
        ],
        out_specs=pl.BlockSpec((rows, tile), lambda c: (0, c)),
        out_shape=jax.ShapeDtypeStruct(vectors.shape, vectors.dtype),
        scratch_shapes=[pltpu.VMEM((rows + 2 * HALO, tile), jnp.float32)],
        name="apply",
    )(q, above, vectors, below)


def solution(mesh):
    placed = (P("row", "col"), P("col", "row"))
    return jax.shard_map(
        shards, mesh=mesh, in_specs=placed, out_specs=P("row", "col"), check_vma=False
    )
```

```python
import functools

import jax
import jax.numpy as jnp
from jax import lax
from jax.experimental import pallas as pl
from jax.experimental.pallas import tpu as pltpu
from jax.sharding import PartitionSpec as P

BAND = 64
GROUPS = 4
WIN = 2 * BAND
HALO = GROUPS * BAND
SIDE = GROUPS // 2


def group_range(group, own):
    return group // 2, own + GROUPS - group


def split(x):
    high = x.astype(jnp.bfloat16)
    low = (x - high.astype(jnp.float32)).astype(jnp.bfloat16)
    return high, low


def dot(a, b, dims=(1, 0)):
    return lax.dot_general(
        a, b, (((dims[0],), (dims[1],)), ((), ())), preferred_element_type=jnp.float32
    )


def product(a, b):
    ah, al = split(a)
    bh, bl = split(b)
    return dot(jnp.concatenate([ah, al], 1), jnp.concatenate([bh, bh], 0)) + dot(ah, bl)


def build_group(own, all_windows, group, refl, q_ref):
    first = lax.axis_index("row") * own - SIDE
    size = WIN
    held = own + 2 * SIDE
    pairs = (held + 1) // 2
    row = lax.broadcasted_iota(jnp.int32, (size, size), 0)
    lane = lax.broadcasted_iota(jnp.int32, (size, size), 1)
    eye = row == lane
    identity = eye.astype(jnp.float32)
    upper = (row // BAND == lane // BAND) & (row < lane)
    inside = (row // BAND) == (lane // BAND)
    lead = inside & (lane % BAND == 0)

    skews, nils, invs, scaled = [], [], [], []
    for pair in range(pairs):
        if (pair + 1) * size <= held * BAND:
            slab = refl[:, pair * size : (pair + 1) * size]
        else:
            part = refl[:, pair * size : pair * size + BAND]
            slab = jnp.concatenate([part, jnp.zeros_like(part)], 1)
        both = jnp.concatenate([slab, slab], 0)
        both = jnp.where(lead, 1.0, jnp.where(inside, both, 0.0))
        skews.append(pltpu.roll(both, 0, 1, stride=1, stride_axis=0))
    for pair in range(pairs):
        high, low = split(skews[pair])
        gram = dot(
            jnp.concatenate([high, low], 1), jnp.concatenate([high, high], 1), (1, 1)
        ) + dot(high, low, (1, 1))
        diag = 0.5 * jnp.sum(jnp.where(eye, gram, 0.0), axis=1, keepdims=True)
        scale = 1.0 / diag
        nils.append(jnp.where(upper, gram * scale, 0.0))
        scaled.append(skews[pair] * scale)
    block = BAND // 4
    near = row // block == lane // block
    powers = [jnp.where(near, n, 0.0) for n in nils]
    invs = [identity - p for p in powers]
    powers = [product(p, p) for p in powers]
    for level in range(2):
        stacked = [product(jnp.concatenate([i, p], 0), p) for i, p in zip(invs, powers)]
        invs = [i + s[:size] for i, s in zip(invs, stacked)]
        powers = [s[size:] for s in stacked]
    invs = [i + product(i, p) for i, p in zip(invs, powers)]
    for _ in range(2):
        wide = row // (2 * block) == lane // (2 * block)
        far = wide & (row // block != lane // block)
        cross = [product(jnp.where(far, n, 0.0), i) for n, i in zip(nils, invs)]
        invs = [i - product(i, c) for i, c in zip(invs, cross)]
        block *= 2
    solved = [product(i, s) for i, s in zip(invs, scaled)]
    usable = all_windows - group % 2
    for pair in range(pairs):
        sh, sl = split(skews[pair])
        th, tl = split(solved[pair])
        for half in range(2):
            k = 2 * pair + half
            if k >= held:
                continue
            at = slice(half * BAND, (half + 1) * BAND)
            left = jnp.concatenate([sh[at], sl[at], sh[at]], 0)
            right = jnp.concatenate([th[at], th[at], tl[at]], 0)
            change = dot(left, right, (0, 0))
            window = first + k
            weight = ((window >= 0) & (window < usable)).astype(jnp.float32)
            high, low = split(identity - weight * change)
            q_ref[group, k, :, :size] = high
            q_ref[group, k, :, size:] = low


def mixed(a, b, count):
    total, bit = 0, 1
    while bit < count:
        total = total + ((a // bit + b // bit) % 2) * bit
        bit *= 2
    return total


def apply_windows(windows, q_ref, work):
    columns = work.shape[1]
    tile = min(columns, 256)

    def one_tile(step, carry):
        cols = pl.ds(pl.multiple_of(step * tile, tile), tile)
        for group, k, at in windows:
            xh, xl = split(work[at : at + WIN, cols])
            q = q_ref[group, k]
            work[at : at + WIN, cols] = dot(q, jnp.concatenate([xh, xh], 0)) + dot(q[:, :WIN], xl)
        return carry

    lax.fori_loop(0, columns // tile, one_tile, 0)


def gather_kernel(
    own, rows_axis, cols_axis, refl_ref, head_ref, tail_ref, x_ref, out_ref,
    q_ref, work, main, left, right, near_send, near_recv, line_send, line_recv, pair_send, pair_recv, own_sem, x_sem, out_sem,
):
    row, me = lax.axis_index("row"), lax.axis_index("col")
    chips = cols_axis // 2
    chip, core = me // 2, me % 2
    up, down = (row + rows_axis - 1) % rows_axis, (row + 1) % rows_axis
    other = chip * 2 + 1 - core
    rows = x_ref.shape[0]
    mesh_ids = pl.DeviceIdType.MESH

    barrier = pltpu.get_barrier_semaphore()
    partners = [(row, mixed(chip, i, chips) * 2 + core) for i in range(1, chips)]
    partners += [(row, other), (up, me), (down, me)]
    for partner in partners:
        pl.semaphore_signal(barrier, inc=1, device_id=partner, device_id_type=mesh_ids)
    pl.semaphore_wait(barrier, len(partners))

    def remote(source, target, send, recv, device):
        return pltpu.make_async_remote_copy(
            src_ref=source, dst_ref=target, send_sem=send, recv_sem=recv,
            device_id=device, device_id_type=mesh_ids,
        )

    slots = (main, left, right)
    pending = []

    def share(kind, source):
        pair = remote(source, slots[kind].at[me], pair_send.at[kind, chip], pair_recv.at[kind, chip], (row, other))
        pair.start()
        pending.append(pair)
        for i in range(1, chips):
            there = mixed(chip, i, chips)
            line = remote(source, slots[kind].at[me], line_send.at[kind, there], line_recv.at[kind, chip], (row, there * 2 + core))
            line.start()
            pending.append(line)

    near = [
        remote(tail_ref, left.at[me], near_send.at[0], near_recv.at[0], (down, me)),
        remote(head_ref, right.at[me], near_send.at[1], near_recv.at[1], (up, me)),
    ]
    for copy in near:
        copy.start()
    halos = [
        remote(x_ref.at[pl.ds(rows - HALO, HALO)], work.at[pl.ds(0, HALO)], near_send.at[2], near_recv.at[2], (down, me)),
        remote(x_ref.at[pl.ds(0, HALO)], work.at[pl.ds(HALO + rows, HALO)], near_send.at[3], near_recv.at[3], (up, me)),
    ]
    for copy in halos:
        copy.start()
    fill = pltpu.make_async_copy(x_ref, work.at[pl.ds(HALO, rows)], x_sem)
    local = pltpu.make_async_copy(refl_ref, main.at[me], own_sem)
    local.start()
    share(0, refl_ref)
    fill.start()
    for kind, copy in zip((1, 2), near):
        copy.wait_recv()
        share(kind, slots[kind].at[me])
    local.wait()

    def arrived(kind, there, mine, recv):
        slot = slots[kind].at[there * 2 + (core if mine else 1 - core)]
        remote(slot, slot, own_sem, recv.at[kind, there], (row, other)).wait_recv()

    share_group = cols_axis // GROUPS
    chip_group = share_group // 2
    mine = chip // chip_group

    def members(i):
        base = mixed(mine, i, GROUPS) * chip_group
        return [base + mixed(chip % chip_group, j, chip_group) for j in range(chip_group)]

    def forward(i):
        for j, there in enumerate(members(i)):
            if i == 0 and j == 0:
                continue
            for kind in range(3):
                arrived(kind, there, True, line_recv)
                slot = slots[kind].at[there * 2 + core]
                copy = remote(slot, slot, pair_send.at[kind, there], pair_recv.at[kind, there], (row, other))
                copy.start()
                pending.append(copy)

    def build(i):
        for there in members(i):
            for kind in range(3):
                arrived(kind, there, False, pair_recv)
        group = mixed(mine, i, GROUPS)
        parts = [slot[pl.ds(group * share_group, share_group)] for slot in (left, main, right)]
        refl = jnp.concatenate([p.reshape(BAND, p.shape[2]) for p in parts], 1)
        build_group(own, own * rows_axis, group, refl, q_ref)

    forward(0)
    build(0)
    forward(1)
    for i in range(1, GROUPS):
        if i + 1 < GROUPS:
            forward(i + 1)
        build(i)
    inner, outer = [], []
    for group in range(GROUPS):
        start, count = group_range(group, own)
        for k in range(start, start + count):
            at = BAND * (group % 2) + WIN * k
            free = at >= HALO + BAND * group and at + WIN <= HALO + rows - BAND * group
            (inner if free else outer).append((group, k, at))

    fill.wait()
    apply_windows(inner, q_ref, work)
    margin = BAND * (GROUPS - 1)

    def result(first, size, at):
        return pltpu.make_async_copy(
            work.at[pl.ds(HALO + first, size)], out_ref.at[pl.ds(first, size)], out_sem.at[at]
        )

    results = [result(margin, rows - 2 * margin, 0), result(0, margin, 1), result(rows - margin, margin, 2)]
    results[0].start()
    for copy in halos:
        copy.wait_recv()
    apply_windows(outer, q_ref, work)
    for copy in results[1:]:
        copy.start()
    for copy in results:
        copy.wait()
    for copy in halos:
        copy.wait_send()
    for copy in near:
        copy.wait_send()
    for copy in pending:
        copy.wait_send()


def shards(vectors, reflectors):
    rows, columns = vectors.shape
    own = rows // WIN
    rows_axis, cols_axis = lax.axis_size("row"), lax.axis_size("col")
    width = SIDE * BAND
    slots, stored = reflectors.shape
    head, tail = reflectors[:, :width], reflectors[:, stored - width :]
    held = own + 2 * SIDE
    anywhere = pl.BlockSpec(memory_space=pl.ANY)
    dma = pltpu.SemaphoreType.DMA
    return pl.pallas_call(
        functools.partial(gather_kernel, own, rows_axis, cols_axis),
        in_specs=[anywhere] * 4,
        out_specs=anywhere,
        out_shape=jax.ShapeDtypeStruct(vectors.shape, vectors.dtype),
        scratch_shapes=[
            pltpu.VMEM((GROUPS, held, WIN, 2 * WIN), jnp.bfloat16),
            pltpu.VMEM((rows + 2 * HALO, columns), jnp.float32),
            pltpu.VMEM((cols_axis, slots, stored), jnp.float32),
            pltpu.VMEM((cols_axis, slots, width), jnp.float32),
            pltpu.VMEM((cols_axis, slots, width), jnp.float32),
            dma((4,)),
            dma((4,)),
            dma((3, cols_axis // 2)),
            dma((3, cols_axis // 2)),
            dma((3, cols_axis // 2)),
            dma((3, cols_axis // 2)),
            dma,
            dma,
            dma((3,)),
        ],
        compiler_params=pltpu.CompilerParams(collective_id=0, has_side_effects=True),
        name="gather",
    )(reflectors, head, tail, vectors)


def solution(mesh):
    placed = (P("row", "col"), P("col", "row"))
    return jax.shard_map(
        shards, mesh=mesh, in_specs=placed, out_specs=P("row", "col"), check_vma=False
    )
```

```python
import functools

import jax
import jax.numpy as jnp
from jax import lax
from jax.experimental import pallas as pl
from jax.experimental.pallas import tpu as pltpu
from jax.sharding import PartitionSpec as P

BAND = 64
GROUPS = 4
WIN = 2 * BAND
HALO = GROUPS * BAND
SIDE = GROUPS // 2


def group_range(group, own):
    return group // 2, own + GROUPS - group


def split(x):
    high = x.astype(jnp.bfloat16)
    low = (x - high.astype(jnp.float32)).astype(jnp.bfloat16)
    return high, low


def dot(a, b, dims=(1, 0)):
    return lax.dot_general(
        a, b, (((dims[0],), (dims[1],)), ((), ())), preferred_element_type=jnp.float32
    )


def product(a, b):
    ah, al = split(a)
    bh, bl = split(b)
    return dot(jnp.concatenate([ah, al], 1), jnp.concatenate([bh, bh], 0)) + dot(ah, bl)


def build_group(own, all_windows, group, refl, q_ref):
    first = lax.axis_index("row") * own - SIDE
    size = WIN
    held = own + 2 * SIDE
    pairs = (held + 1) // 2
    row = lax.broadcasted_iota(jnp.int32, (size, size), 0)
    lane = lax.broadcasted_iota(jnp.int32, (size, size), 1)
    eye = row == lane
    identity = eye.astype(jnp.float32)
    upper = (row // BAND == lane // BAND) & (row < lane)
    inside = (row // BAND) == (lane // BAND)
    lead = inside & (lane % BAND == 0)

    skews, nils, invs, scaled = [], [], [], []
    for pair in range(pairs):
        if (pair + 1) * size <= held * BAND:
            slab = refl[:, pair * size : (pair + 1) * size]
        else:
            part = refl[:, pair * size : pair * size + BAND]
            slab = jnp.concatenate([part, jnp.zeros_like(part)], 1)
        both = jnp.concatenate([slab, slab], 0)
        both = jnp.where(lead, 1.0, jnp.where(inside, both, 0.0))
        skews.append(pltpu.roll(both, 0, 1, stride=1, stride_axis=0))
    for pair in range(pairs):
        high, low = split(skews[pair])
        gram = dot(
            jnp.concatenate([high, low], 1), jnp.concatenate([high, high], 1), (1, 1)
        ) + dot(high, low, (1, 1))
        diag = 0.5 * jnp.sum(jnp.where(eye, gram, 0.0), axis=1, keepdims=True)
        scale = 1.0 / diag
        nils.append(jnp.where(upper, gram * scale, 0.0))
        scaled.append(skews[pair] * scale)
    block = BAND // 4
    near = row // block == lane // block
    powers = [jnp.where(near, n, 0.0) for n in nils]
    invs = [identity - p for p in powers]
    powers = [product(p, p) for p in powers]
    for level in range(2):
        stacked = [product(jnp.concatenate([i, p], 0), p) for i, p in zip(invs, powers)]
        invs = [i + s[:size] for i, s in zip(invs, stacked)]
        powers = [s[size:] for s in stacked]
    invs = [i + product(i, p) for i, p in zip(invs, powers)]
    for _ in range(2):
        wide = row // (2 * block) == lane // (2 * block)
        far = wide & (row // block != lane // block)
        cross = [product(jnp.where(far, n, 0.0), i) for n, i in zip(nils, invs)]
        invs = [i - product(i, c) for i, c in zip(invs, cross)]
        block *= 2
    solved = [product(i, s) for i, s in zip(invs, scaled)]
    usable = all_windows - group % 2
    for pair in range(pairs):
        sh, sl = split(skews[pair])
        th, tl = split(solved[pair])
        for half in range(2):
            k = 2 * pair + half
            if k >= held:
                continue
            at = slice(half * BAND, (half + 1) * BAND)
            left = jnp.concatenate([sh[at], sl[at], sh[at]], 0)
            right = jnp.concatenate([th[at], th[at], tl[at]], 0)
            change = dot(left, right, (0, 0))
            window = first + k
            weight = ((window >= 0) & (window < usable)).astype(jnp.float32)
            high, low = split(identity - weight * change)
            q_ref[group, k, :, :size] = high
            q_ref[group, k, :, size:] = low


def mixed(a, b, count):
    total, bit = 0, 1
    while bit < count:
        total = total + ((a // bit + b // bit) % 2) * bit
        bit *= 2
    return total


def apply_windows(windows, q_ref, work):
    columns = work.shape[1]
    tile = min(columns, 256)

    def one_tile(step, carry):
        cols = pl.ds(pl.multiple_of(step * tile, tile), tile)
        for group, k, at in windows:
            xh, xl = split(work[at : at + WIN, cols])
            q = q_ref[group, k]
            work[at : at + WIN, cols] = dot(q, jnp.concatenate([xh, xh], 0)) + dot(q[:, :WIN], xl)
        return carry

    lax.fori_loop(0, columns // tile, one_tile, 0)


def gather_kernel(
    own, rows_axis, cols_axis, refl_ref, tail_ref, x_ref, out_ref,
    q_ref, work, main, left, right, near_send, near_recv, line_send, line_recv, pair_send, pair_recv, own_sem, x_sem, out_sem,
):
    row, me = lax.axis_index("row"), lax.axis_index("col")
    chips = cols_axis // 2
    chip, core = me // 2, me % 2
    up, down = (row + rows_axis - 1) % rows_axis, (row + 1) % rows_axis
    other = chip * 2 + 1 - core
    rows = x_ref.shape[0]
    mesh_ids = pl.DeviceIdType.MESH

    barrier = pltpu.get_barrier_semaphore()
    partners = [(row, mixed(chip, i, chips) * 2 + core) for i in range(1, chips)]
    partners += [(row, other), (up, me), (down, me)]
    for partner in partners:
        pl.semaphore_signal(barrier, inc=1, device_id=partner, device_id_type=mesh_ids)
    pl.semaphore_wait(barrier, len(partners))

    def remote(source, target, send, recv, device):
        return pltpu.make_async_remote_copy(
            src_ref=source, dst_ref=target, send_sem=send, recv_sem=recv,
            device_id=device, device_id_type=mesh_ids,
        )

    slots = (main, left, right)
    pending = []

    def share(kind, source):
        pair = remote(source, slots[kind].at[me], pair_send.at[kind, chip], pair_recv.at[kind, chip], (row, other))
        pair.start()
        pending.append(pair)
        for i in range(1, chips):
            there = mixed(chip, i, chips)
            line = remote(source, slots[kind].at[me], line_send.at[kind, there], line_recv.at[kind, chip], (row, there * 2 + core))
            line.start()
            pending.append(line)

    near = [
        remote(tail_ref, left.at[me], near_send.at[0], near_recv.at[0], (down, me)),
        remote(refl_ref.at[:, pl.ds(0, right.shape[2])], right.at[me], near_send.at[1], near_recv.at[1], (up, me)),
    ]
    for copy in near:
        copy.start()
    half = HALO // 2
    halos = []
    for part, offset in enumerate((half, 0)):
        above = (x_ref.at[pl.ds(rows - HALO + offset, half)], work.at[pl.ds(offset, half)])
        below = (x_ref.at[pl.ds(half - offset, half)], work.at[pl.ds(HALO + rows + half - offset, half)])
        at = 2 + 2 * part
        halos.append(remote(*above, near_send.at[at], near_recv.at[at], (down, me)))
        halos.append(remote(*below, near_send.at[at + 1], near_recv.at[at + 1], (up, me)))
    for copy in halos:
        copy.start()
    fill = pltpu.make_async_copy(x_ref, work.at[pl.ds(HALO, rows)], x_sem)
    local = pltpu.make_async_copy(refl_ref, main.at[me], own_sem)
    local.start()
    share(0, refl_ref)
    fill.start()
    for kind, copy in zip((1, 2), near):
        copy.wait_recv()
        share(kind, slots[kind].at[me])
    local.wait()

    def arrived(kind, there, mine, recv):
        slot = slots[kind].at[there * 2 + (core if mine else 1 - core)]
        remote(slot, slot, own_sem, recv.at[kind, there], (row, other)).wait_recv()

    share_group = cols_axis // GROUPS
    chip_group = share_group // 2
    mine = chip // chip_group

    def members(i):
        base = mixed(mine, i, GROUPS) * chip_group
        return [base + mixed(chip % chip_group, j, chip_group) for j in range(chip_group)]

    def forward(i):
        for j, there in enumerate(members(i)):
            if i == 0 and j == 0:
                continue
            for kind in range(3):
                arrived(kind, there, True, line_recv)
                slot = slots[kind].at[there * 2 + core]
                copy = remote(slot, slot, pair_send.at[kind, there], pair_recv.at[kind, there], (row, other))
                copy.start()
                pending.append(copy)

    def build(i):
        for there in members(i):
            for kind in range(3):
                arrived(kind, there, False, pair_recv)
        group = mixed(mine, i, GROUPS)
        parts = [slot[pl.ds(group * share_group, share_group)] for slot in (left, main, right)]
        refl = jnp.concatenate([p.reshape(BAND, p.shape[2]) for p in parts], 1)
        build_group(own, own * rows_axis, group, refl, q_ref)

    forward(0)
    build(0)
    forward(1)
    for i in range(1, GROUPS):
        if i + 1 < GROUPS:
            forward(i + 1)
        build(i)
    parts = ([], [], [])
    for group in range(GROUPS):
        start, count = group_range(group, own)
        for k in range(start, start + count):
            at = BAND * (group % 2) + WIN * k
            for part, reach in enumerate((0, half, HALO)):
                low = HALO - reach + BAND * group
                if at >= low and at + WIN <= 2 * HALO + rows - low:
                    parts[part].append((group, k, at))
                    break

    fill.wait()
    apply_windows(parts[0], q_ref, work)
    margin = BAND * (GROUPS - 1)
    nearer = margin - half

    def result(first, size, at):
        return pltpu.make_async_copy(
            work.at[pl.ds(HALO + first, size)], out_ref.at[pl.ds(first, size)], out_sem.at[at]
        )

    results = [
        result(margin, rows - 2 * margin, 0),
        result(nearer, half, 1),
        result(rows - margin, half, 2),
        result(0, nearer, 3),
        result(rows - nearer, nearer, 4),
    ]
    results[0].start()
    for part in range(2):
        for copy in halos[2 * part : 2 * part + 2]:
            copy.wait_recv()
        apply_windows(parts[1 + part], q_ref, work)
        for copy in results[1 + 2 * part : 3 + 2 * part]:
            copy.start()
    for copy in results:
        copy.wait()
    for copy in halos:
        copy.wait_send()
    for copy in near:
        copy.wait_send()
    for copy in pending:
        copy.wait_send()


def shards(vectors, reflectors):
    rows, columns = vectors.shape
    own = rows // WIN
    rows_axis, cols_axis = lax.axis_size("row"), lax.axis_size("col")
    width = SIDE * BAND
    slots, stored = reflectors.shape
    tail = reflectors[:, stored - width :]
    held = own + 2 * SIDE
    anywhere = pl.BlockSpec(memory_space=pl.ANY)
    dma = pltpu.SemaphoreType.DMA
    return pl.pallas_call(
        functools.partial(gather_kernel, own, rows_axis, cols_axis),
        in_specs=[pl.BlockSpec(memory_space=pltpu.HBM)] * 3,
        out_specs=anywhere,
        out_shape=jax.ShapeDtypeStruct(vectors.shape, vectors.dtype),
        scratch_shapes=[
            pltpu.VMEM((GROUPS, held, WIN, 2 * WIN), jnp.bfloat16),
            pltpu.VMEM((rows + 2 * HALO, columns), jnp.float32),
            pltpu.VMEM((cols_axis, slots, stored), jnp.float32),
            pltpu.VMEM((cols_axis, slots, width), jnp.float32),
            pltpu.VMEM((cols_axis, slots, width), jnp.float32),
            dma((6,)),
            dma((6,)),
            dma((3, cols_axis // 2)),
            dma((3, cols_axis // 2)),
            dma((3, cols_axis // 2)),
            dma((3, cols_axis // 2)),
            dma,
            dma,
            dma((5,)),
        ],
        compiler_params=pltpu.CompilerParams(collective_id=0, has_side_effects=True, vmem_limit_bytes=24 * 2**20),
        name="gather",
    )(reflectors, tail, vectors)


def solution(mesh):
    placed = (P("row", "col"), P("col", "row"))
    return jax.shard_map(
        shards, mesh=mesh, in_specs=placed, out_specs=P("row", "col"), check_vma=False
    )
```

```python
import functools

import jax
import jax.numpy as jnp
from jax import lax
from jax.experimental import pallas as pl
from jax.experimental.pallas import tpu as pltpu
from jax.sharding import PartitionSpec as P

BAND = 64
GROUPS = 4
WIN = 2 * BAND
HALO = GROUPS * BAND
SIDE = GROUPS // 2


def group_range(group, own):
    return group // 2, own + GROUPS - group


def split(x):
    high = x.astype(jnp.bfloat16)
    low = (x - high.astype(jnp.float32)).astype(jnp.bfloat16)
    return high, low


def dot(a, b, dims=(1, 0)):
    return lax.dot_general(
        a, b, (((dims[0],), (dims[1],)), ((), ())), preferred_element_type=jnp.float32
    )


def product(a, b):
    ah, al = split(a)
    bh, bl = split(b)
    return dot(jnp.concatenate([ah, al], 1), jnp.concatenate([bh, bh], 0)) + dot(ah, bl)


def build_group(own, all_windows, group, refl, q_ref):
    first = lax.axis_index("row") * own - SIDE
    size = WIN
    held = own + 2 * SIDE
    pairs = (held + 1) // 2
    row = lax.broadcasted_iota(jnp.int32, (size, size), 0)
    lane = lax.broadcasted_iota(jnp.int32, (size, size), 1)
    eye = row == lane
    identity = eye.astype(jnp.float32)
    upper = (row // BAND == lane // BAND) & (row < lane)
    inside = (row // BAND) == (lane // BAND)
    lead = inside & (lane % BAND == 0)

    skews, nils, invs, scaled = [], [], [], []
    for pair in range(pairs):
        if (pair + 1) * size <= held * BAND:
            slab = refl[:, pair * size : (pair + 1) * size]
        else:
            part = refl[:, pair * size : pair * size + BAND]
            slab = jnp.concatenate([part, jnp.zeros_like(part)], 1)
        both = jnp.concatenate([slab, slab], 0)
        both = jnp.where(lead, 1.0, jnp.where(inside, both, 0.0))
        skews.append(pltpu.roll(both, 0, 1, stride=1, stride_axis=0))
    for pair in range(pairs):
        high, low = split(skews[pair])
        gram = dot(
            jnp.concatenate([high, low], 1), jnp.concatenate([high, high], 1), (1, 1)
        ) + dot(high, low, (1, 1))
        diag = 0.5 * jnp.sum(jnp.where(eye, gram, 0.0), axis=1, keepdims=True)
        scale = 1.0 / diag
        nils.append(jnp.where(upper, gram * scale, 0.0))
        scaled.append(skews[pair] * scale)
    block = BAND // 4
    near = row // block == lane // block
    powers = [jnp.where(near, n, 0.0) for n in nils]
    invs = [identity - p for p in powers]
    powers = [product(p, p) for p in powers]
    for level in range(2):
        stacked = [product(jnp.concatenate([i, p], 0), p) for i, p in zip(invs, powers)]
        invs = [i + s[:size] for i, s in zip(invs, stacked)]
        powers = [s[size:] for s in stacked]
    invs = [i + product(i, p) for i, p in zip(invs, powers)]
    for _ in range(2):
        wide = row // (2 * block) == lane // (2 * block)
        far = wide & (row // block != lane // block)
        cross = [product(jnp.where(far, n, 0.0), i) for n, i in zip(nils, invs)]
        invs = [i - product(i, c) for i, c in zip(invs, cross)]
        block *= 2
    solved = [product(i, s) for i, s in zip(invs, scaled)]
    usable = all_windows - group % 2
    for pair in range(pairs):
        sh, sl = split(skews[pair])
        th, tl = split(solved[pair])
        for half in range(2):
            k = 2 * pair + half
            if k >= held:
                continue
            at = slice(half * BAND, (half + 1) * BAND)
            left = jnp.concatenate([sh[at], sl[at], sh[at]], 0)
            right = jnp.concatenate([th[at], th[at], tl[at]], 0)
            change = dot(left, right, (0, 0))
            window = first + k
            weight = ((window >= 0) & (window < usable)).astype(jnp.float32)
            high, low = split(identity - weight * change)
            q_ref[group, k, :, :size] = high
            q_ref[group, k, :, size:] = low


def mixed(a, b, count):
    total, bit = 0, 1
    while bit < count:
        total = total + ((a // bit + b // bit) % 2) * bit
        bit *= 2
    return total


def apply_windows(windows, q_ref, work):
    columns = work.shape[1]
    tile = min(columns, 256)

    def one_tile(step, carry):
        cols = pl.ds(pl.multiple_of(step * tile, tile), tile)
        for group, k, at in windows:
            xh, xl = split(work[at : at + WIN, cols])
            q = q_ref[group, k]
            work[at : at + WIN, cols] = dot(q, jnp.concatenate([xh, xh], 0)) + dot(q[:, :WIN], xl)
        return carry

    lax.fori_loop(0, columns // tile, one_tile, 0)


def gather_kernel(
    own, rows_axis, cols_axis, refl_ref, tail_ref, x_ref, out_ref,
    q_ref, work, main, left, right, near_send, near_recv, line_send, line_recv, pair_send, pair_recv, own_sem, x_sem, out_sem,
):
    row, me = lax.axis_index("row"), lax.axis_index("col")
    chips = cols_axis // 2
    chip, core = me // 2, me % 2
    up, down = (row + rows_axis - 1) % rows_axis, (row + 1) % rows_axis
    other = chip * 2 + 1 - core
    rows = x_ref.shape[0]
    mesh_ids = pl.DeviceIdType.MESH

    barrier = pltpu.get_barrier_semaphore()
    partners = [(row, mixed(chip, i, chips) * 2 + core) for i in range(1, chips)]
    partners += [(row, other), (up, me), (down, me)]
    for partner in partners:
        pl.semaphore_signal(barrier, inc=1, device_id=partner, device_id_type=mesh_ids)
    pl.semaphore_wait(barrier, len(partners))

    def remote(source, target, send, recv, device):
        return pltpu.make_async_remote_copy(
            src_ref=source, dst_ref=target, send_sem=send, recv_sem=recv,
            device_id=device, device_id_type=mesh_ids,
        )

    slots = (main, left, right)
    pending = []

    def share(kind, source):
        pair = remote(source, slots[kind].at[me], pair_send.at[kind, chip], pair_recv.at[kind, chip], (row, other))
        pair.start()
        pending.append(pair)
        for i in range(1, chips):
            there = mixed(chip, i, chips)
            line = remote(source, slots[kind].at[me], line_send.at[kind, there], line_recv.at[kind, chip], (row, there * 2 + core))
            line.start()
            pending.append(line)

    near = [
        remote(tail_ref, left.at[me], near_send.at[0], near_recv.at[0], (down, me)),
        remote(refl_ref.at[:, pl.ds(0, right.shape[2])], right.at[me], near_send.at[1], near_recv.at[1], (up, me)),
    ]
    for copy in near:
        copy.start()
    half = HALO // 2
    halos = []
    for part, offset in enumerate((half, 0)):
        above = (x_ref.at[pl.ds(rows - HALO + offset, half)], work.at[pl.ds(offset, half)])
        below = (x_ref.at[pl.ds(half - offset, half)], work.at[pl.ds(HALO + rows + half - offset, half)])
        at = 2 + 2 * part
        halos.append(remote(*above, near_send.at[at], near_recv.at[at], (down, me)))
        halos.append(remote(*below, near_send.at[at + 1], near_recv.at[at + 1], (up, me)))
    for copy in halos:
        copy.start()
    fill = pltpu.make_async_copy(x_ref, work.at[pl.ds(HALO, rows)], x_sem)
    local = pltpu.make_async_copy(refl_ref, main.at[me], own_sem)
    local.start()
    share(0, refl_ref)
    fill.start()
    for kind, copy in zip((1, 2), near):
        copy.wait_recv()
        share(kind, slots[kind].at[me])
    local.wait()

    def arrived(kind, there, mine, recv):
        slot = slots[kind].at[there * 2 + (core if mine else 1 - core)]
        remote(slot, slot, own_sem, recv.at[kind, there], (row, other)).wait_recv()

    share_group = cols_axis // GROUPS
    chip_group = share_group // 2
    mine = chip // chip_group

    def members(i):
        base = mixed(mine, i, GROUPS) * chip_group
        return [base + mixed(chip % chip_group, j, chip_group) for j in range(chip_group)]

    def forward(i):
        for j, there in enumerate(members(i)):
            if i == 0 and j == 0:
                continue
            for kind in range(3):
                arrived(kind, there, True, line_recv)
                slot = slots[kind].at[there * 2 + core]
                copy = remote(slot, slot, pair_send.at[kind, there], pair_recv.at[kind, there], (row, other))
                copy.start()
                pending.append(copy)

    def build(i):
        for there in members(i):
            for kind in range(3):
                arrived(kind, there, False, pair_recv)
        group = mixed(mine, i, GROUPS)
        parts = [slot[pl.ds(group * share_group, share_group)] for slot in (left, main, right)]
        refl = jnp.concatenate([p.reshape(BAND, p.shape[2]) for p in parts], 1)
        build_group(own, own * rows_axis, group, refl, q_ref)

    forward(0)
    build(0)
    forward(1)
    for i in range(1, GROUPS):
        if i + 1 < GROUPS:
            forward(i + 1)
        build(i)
    parts = ([], [], [])
    for group in range(GROUPS):
        start, count = group_range(group, own)
        for k in range(start, start + count):
            at = BAND * (group % 2) + WIN * k
            for part, reach in enumerate((0, half, HALO)):
                low = HALO - reach + BAND * group
                if at >= low and at + WIN <= 2 * HALO + rows - low:
                    parts[part].append((group, k, at))
                    break

    fill.wait()
    apply_windows(parts[0], q_ref, work)
    margin = BAND * (GROUPS - 1)
    nearer = margin - half

    def result(first, size, at):
        return pltpu.make_async_copy(
            work.at[pl.ds(HALO + first, size)], out_ref.at[pl.ds(first, size)], out_sem.at[at]
        )

    results = [
        result(margin, rows - 2 * margin, 0),
        result(nearer, half, 1),
        result(rows - margin, half, 2),
        result(0, nearer, 3),
        result(rows - nearer, nearer, 4),
    ]
    results[0].start()
    for part in range(2):
        for copy in halos[2 * part : 2 * part + 2]:
            copy.wait_recv()
        apply_windows(parts[1 + part], q_ref, work)
        for copy in results[1 + 2 * part : 3 + 2 * part]:
            copy.start()
    for copy in results:
        copy.wait()
    for copy in halos:
        copy.wait_send()
    for copy in near:
        copy.wait_send()
    for copy in pending:
        copy.wait_send()


def shards(vectors, reflectors):
    rows, columns = vectors.shape
    own = rows // WIN
    rows_axis, cols_axis = lax.axis_size("row"), lax.axis_size("col")
    width = SIDE * BAND
    slots, stored = reflectors.shape
    tail = reflectors[:, stored - width :]
    held = own + 2 * SIDE
    anywhere = pl.BlockSpec(memory_space=pl.ANY)
    dma = pltpu.SemaphoreType.DMA
    return pl.pallas_call(
        functools.partial(gather_kernel, own, rows_axis, cols_axis),
        in_specs=[pl.BlockSpec(memory_space=pltpu.HBM)] * 3,
        out_specs=anywhere,
        out_shape=jax.ShapeDtypeStruct(vectors.shape, vectors.dtype),
        scratch_shapes=[
            pltpu.VMEM((GROUPS, held, WIN, 2 * WIN), jnp.bfloat16),
            pltpu.VMEM((rows + 2 * HALO, columns), jnp.float32),
            pltpu.VMEM((cols_axis, slots, stored), jnp.float32),
            pltpu.VMEM((cols_axis, slots, width), jnp.float32),
            pltpu.VMEM((cols_axis, slots, width), jnp.float32),
            dma((6,)),
            dma((6,)),
            dma((3, cols_axis // 2)),
            dma((3, cols_axis // 2)),
            dma((3, cols_axis // 2)),
            dma((3, cols_axis // 2)),
            dma,
            dma,
            dma((5,)),
        ],
        compiler_params=pltpu.CompilerParams(collective_id=0, has_side_effects=True, vmem_limit_bytes=50 * 2**20),
        name="gather",
    )(reflectors, tail, vectors)


def solution(mesh):
    placed = (P("row", "col"), P("col", "row"))
    return jax.shard_map(
        shards, mesh=mesh, in_specs=placed, out_specs=P("row", "col"), check_vma=False
    )
```
